32 devices in a mesh: dp: 4 (over y, core), feat: 8 (over z, x).
Axes of the slice: x: 2, y: 2, z: 4, core: 2. Of those that a mesh axis runs over, the one named last changes fastest.
Arguments:
- images: bfloat16 [1536, 3072], P('dp'), may hold values from -6 to 6
- labels: int32 [1536], P('dp'), may hold values from 0 to 9
- frequencies: bfloat16 [3072, 8192], P(None, 'feat'), may hold values from -0.15625 to 0.15625
- privacy_noise: float32 [10, 2, 8192], P(None, None, 'feat'), may hold values from -0.6 to 0.6
- latents: bfloat16 [1024, 256], P('dp'), may hold values from -6 to 6
- gen_labels: int32 [1024], P('dp'), may hold values from 0 to 9
- gen_in: bfloat16 [256, 1024], replicated, may hold values from -0.375 to 0.375
- gen_out: bfloat16 [1024, 3072], replicated, may hold values from -0.25 to 0.25
Outputs:
- match_loss: float32 [], replicated
- grad_in: float32 [256, 1024], P('dp')
- grad_out: float32 [1024, 3072], P('dp')
The draws below stay inside these ranges and needn't reach their ends.
All inputs are finite; a program needn't handle non-finite values.
Results may differ from the reference program's by a relative error of at most 0.0035.
Values sent between devices are 32-bit elements; how exact they have to be, the bound alone decides.
No kernel may reach another device: no remote copies, remote signals or barrier semaphores. Data moves between devices by JAX's collectives and lax.ppermute only.
A program may use at most 128 MiB of HBM per device.

```python
import jax
import jax.numpy as jnp
from jax import lax

D = 3072
CLASSES = 10
HID = 1024
ZDIM = 256
IMAGES = 1536
GEN = 1024
FEATS = 8192


def set_ends(values, own_key, smallest, largest):
    spot = [jax.random.randint(jax.random.fold_in(own_key, axis), (), 0, length) for axis, length in enumerate(values.shape)]
    widest = values.shape.index(max(values.shape))
    neighbour = spot[:widest] + [(spot[widest] + 1) % values.shape[widest]] + spot[widest + 1:]
    return values.at[tuple(spot)].set(smallest).at[tuple(neighbour)].set(largest)


def shard_levels(stream_key, shape, shards, smallest, high):
    def one(dim, parts):
        steps = jax.random.uniform(jax.random.fold_in(jax.random.fold_in(stream_key, 6), dim), (parts,), jnp.float32, smallest / len(shards), high / len(shards))
        return jnp.repeat(jnp.exp(steps), shape[dim] // parts).reshape((-1,) + (1,) * (len(shape) - dim - 1))

    factor_of = one(*shards[0])
    for cut in shards[1:]:
        factor_of = factor_of * one(*cut)
    return factor_of


def gaussian(key, extent, scale, most, pieces=(), held_as=jnp.bfloat16):
    gain = shard_levels(key, extent, pieces, -0.22, 0.18) if pieces else 1.0
    array = jax.random.normal(key, extent, jnp.float32) * scale * gain
    return jnp.minimum(jnp.maximum(array, -most), most).astype(held_as)


def setup_inputs(seed: int = 0) -> dict:
    splits = jax.random.split(jax.random.key(seed), 9)
    return {
        "images": gaussian(splits[0], (IMAGES, D), 1.0, 6.0, ((0, 4),)),
        "labels": set_ends(jax.random.randint(splits[1], (IMAGES,), 0, CLASSES), jax.random.fold_in(splits[1], 1), 0, CLASSES - 1).astype(jnp.int32),
        "frequencies": gaussian(splits[2], (D, FEATS), (D // 2) ** -0.5, 0.15625, ((1, 8),)),
        "privacy_noise": gaussian(splits[3], (CLASSES, 2, FEATS), 0.1, 0.6, ((2, 8),), jnp.float32),
        "latents": gaussian(splits[4], (GEN, ZDIM), 1.0, 6.0, ((0, 4),)),
        "gen_labels": set_ends(jax.random.randint(splits[5], (GEN,), 0, CLASSES), jax.random.fold_in(splits[5], 1), 0, CLASSES - 1).astype(jnp.int32),
        "gen_in": gaussian(splits[6], (ZDIM, HID), ZDIM ** -0.5, 0.375),
        "gen_out": gaussian(splits[7], (HID, D), (HID // 2) ** -0.5, 0.25),
    }


def class_means(phase, classes_of, count):
    feats = jnp.concatenate([jnp.cos(phase), jnp.sin(phase)], axis=1)
    onehot = (classes_of[:, None] == jnp.arange(CLASSES)[None, :]).astype(jnp.float32)
    sums = jnp.dot(onehot.T, feats, precision=lax.Precision.HIGHEST) * (CLASSES / count)
    return sums.reshape(CLASSES, 2, FEATS), onehot


def reference(images, labels, frequencies, privacy_noise, latents, gen_labels, gen_in, gen_out):
    data_phase = jnp.dot(images, frequencies, preferred_element_type=jnp.float32)
    data_mean, unused = class_means(data_phase, labels, IMAGES)
    pre_hidden = jnp.dot(latents, gen_in, preferred_element_type=jnp.float32)
    sigmoid_h = jax.nn.sigmoid(pre_hidden)
    hidden = (pre_hidden * sigmoid_h).astype(jnp.bfloat16)
    image_out = jnp.tanh(jnp.dot(hidden, gen_out, preferred_element_type=jnp.float32))
    gen_image = image_out.astype(jnp.bfloat16)
    gen_phase = jnp.dot(gen_image, frequencies, preferred_element_type=jnp.float32)
    gen_mean, gen_onehot = class_means(gen_phase, gen_labels, GEN)
    mean_gap = gen_mean - (data_mean + privacy_noise)
    match_loss = jnp.sum(mean_gap * mean_gap) / (2.0 * FEATS)
    gap_rows = jnp.dot(gen_onehot, mean_gap.reshape(CLASSES, 2 * FEATS), precision=lax.Precision.HIGHEST) * (16.0 * CLASSES / GEN)
    phase_grad = (jnp.cos(gen_phase) * gap_rows[:, FEATS:] - jnp.sin(gen_phase) * gap_rows[:, :FEATS]).astype(jnp.bfloat16)
    image_grad = jnp.dot(phase_grad, frequencies.T, preferred_element_type=jnp.float32)
    out_grad = (image_grad * (1.0 - image_out * image_out)).astype(jnp.bfloat16)
    grad_out = jnp.dot(hidden.T, out_grad, preferred_element_type=jnp.float32)
    back_hidden = jnp.dot(out_grad, gen_out.T, preferred_element_type=jnp.float32)
    hidden_grad = (back_hidden * sigmoid_h * (1.0 + pre_hidden * (1.0 - sigmoid_h))).astype(jnp.bfloat16)
    grad_in = jnp.dot(latents.T, hidden_grad, preferred_element_type=jnp.float32)
    return match_loss, grad_in, grad_out
```

```python
import jax
import jax.numpy as jnp
from jax import lax
from jax.sharding import PartitionSpec as P

F32 = jnp.float32
BF16 = jnp.bfloat16


def swap(x, axis, bit):
    size = lax.axis_size(axis)
    return lax.ppermute(x, axis, [(i, i ^ bit) for i in range(size)])


def bits_of(axis):
    size = lax.axis_size(axis)
    assert size & (size - 1) == 0
    return [1 << k for k in range(size.bit_length() - 1)]


def all_sum(x, axis):
    for bit in bits_of(axis):
        x = x + swap(x, axis, bit)
    return x


def reduce_scatter(parts, axis):
    live = dict(enumerate(parts))
    for bit in bits_of(axis):
        for j in sorted((j for j in live if j & bit), reverse=True):
            got = swap(live.pop(j), axis, bit)
            live[j ^ bit] = live[j ^ bit] + got
    return live[0]


def all_gather(x, axis):
    got = {0: x}
    for bit in reversed(bits_of(axis)):
        for j in sorted(got):
            got[j | bit] = swap(got[j], axis, bit)
    return [got[j] for j in range(len(got))]


def two_term_dot(a, b, dims):
    high = b.astype(BF16)
    low = (b - high.astype(F32)).astype(BF16)
    dot = lambda t: lax.dot_general(a, t, (dims, ((), ())), preferred_element_type=F32)
    return dot(high) + dot(low)


def class_sums(phase, classes_of, classes, scale):
    feats = jnp.concatenate([jnp.cos(phase), jnp.sin(phase)], axis=1)
    onehot = (classes_of[:, None] == jnp.arange(classes)[None, :]).astype(F32)
    return jnp.dot(onehot.T, feats, precision=lax.Precision.HIGHEST) * scale, onehot


def per_device(images, labels, frequencies, privacy_noise, latents, gen_labels, gen_in, gen_out):
    classes = privacy_noise.shape[0]
    feat_dev = frequencies.shape[1]
    nd, nf = lax.axis_size("dp"), lax.axis_size("feat")
    me_d, me_f = lax.axis_index("dp"), lax.axis_index("feat")
    total_images = images.shape[0] * nd
    total_gen = latents.shape[0] * nd
    total_feats = feat_dev * nf
    width = frequencies.shape[0] // nf
    hid_dev, z_dev = gen_in.shape[1] // nd, gen_in.shape[0] // nd

    pre_hidden = jnp.dot(latents, gen_in, preferred_element_type=F32)
    sigmoid_h = jax.nn.sigmoid(pre_hidden)
    hidden = (pre_hidden * sigmoid_h).astype(BF16)
    image_out = jnp.tanh(jnp.dot(hidden, gen_out, preferred_element_type=F32))
    gen_image = image_out.astype(BF16)
    gen_phase = jnp.dot(gen_image, frequencies, preferred_element_type=F32)
    gen_part, gen_onehot = class_sums(gen_phase, gen_labels, classes, classes / total_gen)
    data_phase = jnp.dot(images, frequencies, preferred_element_type=F32)
    data_part, unused = class_sums(data_phase, labels, classes, classes / total_images)

    noise = privacy_noise.reshape(classes, 2 * feat_dev)
    mean_gap = all_sum(gen_part - data_part, "dp") - noise
    loss_part = jnp.sum(mean_gap * mean_gap)
    gap_rows = jnp.dot(gen_onehot, mean_gap, precision=lax.Precision.HIGHEST) * (
        16.0 * classes / total_gen
    )
    phase_grad = (
        jnp.cos(gen_phase) * gap_rows[:, feat_dev:] - jnp.sin(gen_phase) * gap_rows[:, :feat_dev]
    ).astype(BF16)

    def image_part(j):
        rows = lax.dynamic_slice_in_dim(frequencies, (me_f ^ j) * width, width, 0)
        return lax.dot_general(
            phase_grad, rows, (((1,), (1,)), ((), ())), preferred_element_type=F32
        )

    image_grad = reduce_scatter([image_part(j) for j in range(nf)], "feat")

    own_out = lax.dynamic_slice_in_dim(image_out, me_f * width, width, 1)
    own_gen_out = lax.dynamic_slice_in_dim(gen_out, me_f * width, width, 1)
    out_grad = (image_grad * (1.0 - own_out * own_out)).astype(BF16)

    def columns(x, size, j):
        return lax.dynamic_slice_in_dim(x, (me_d ^ j) * size, size, 1)

    def hidden_part(j):
        return lax.dot_general(
            columns(hidden, hid_dev, j), out_grad, (((0,), (0,)), ((), ())), preferred_element_type=F32
        )

    own_rows = reduce_scatter([hidden_part(j) for j in range(nd)], "dp")

    back_hidden = lax.dot_general(
        out_grad, own_gen_out, (((1,), (1,)), ((), ())), preferred_element_type=F32
    )
    hidden_grad = back_hidden * sigmoid_h * (1.0 + pre_hidden * (1.0 - sigmoid_h))
    in_parts = [two_term_dot(columns(latents, z_dev, j), hidden_grad, ((0,), (0,))) for j in range(nd)]
    in_rows = reduce_scatter(in_parts, "dp")
    riders = jnp.zeros((8, in_rows.shape[1]), F32) + loss_part
    in_sum = all_sum(jnp.concatenate([in_rows, riders], axis=0), "feat")
    grad_in = in_sum[:z_dev]
    match_loss = in_sum[z_dev, 0] / (2.0 * total_feats)

    gathered = all_gather(own_rows, "feat")
    grad_out = jnp.zeros((hid_dev, frequencies.shape[0]), F32)
    for j, block in enumerate(gathered):
        grad_out = lax.dynamic_update_slice_in_dim(grad_out, block, (me_f ^ j) * width, 1)
    return (match_loss, grad_in, grad_out)


def solution(mesh):
    return jax.shard_map(
        per_device,
        mesh=mesh,
        in_specs=(
            P("dp", None),
            P("dp"),
            P(None, "feat"),
            P(None, None, "feat"),
            P("dp", None),
            P("dp"),
            P(),
            P(),
        ),
        out_specs=(P(), P("dp", None), P("dp", None)),
        check_vma=False,
    )
```
